32 devices in a mesh: box: 8 (over y, x, core), dir: 4 (over z).
Axes of the slice: x: 2, y: 2, z: 4, core: 2. Of those that a mesh axis runs over, the one named last changes fastest.
Arguments:
- low_field: float32 [2048, 2, 64, 128], P('box', None, 'dir'), may hold values from -6 to 6
- far_src_low: int32 [2048, 8], P('box'), may hold values from -1 to 2047, as said below
- far_class_low: int32 [2048, 8], P('box'), may hold values from 0 to 15
- table_low: float32 [16, 2, 64, 128], P(None, None, 'dir'), may hold values from -3 to 3
- far_src_mid: int32 [256, 8], P('box'), may hold values from -1 to 255, as said below
- far_class_mid: int32 [256, 8], P('box'), may hold values from 0 to 15
- table_mid: float32 [16, 2, 128, 256], P(None, None, 'dir'), may hold values from -3 to 3
- far_src_top: int32 [32, 8], P('box'), may hold values from -1 to 31, as said below
- far_class_top: int32 [32, 8], P('box'), may hold values from 0 to 15
- table_top: float32 [16, 2, 256, 512], P(None, None, 'dir'), may hold values from -3 to 3
Outputs:
- incoming_low: float32 [2048, 2, 64, 128], P('box', None, 'dir')
- incoming_mid: float32 [256, 2, 128, 256], P('box', None, 'dir')
- incoming_top: float32 [32, 2, 256, 512], P('box', None, 'dir')
The draws below stay inside these ranges and needn't reach their ends.
Inputs may be any that keep to these rules, and one draw needn't show every extreme that they name: `far_src_low`: each box has 8 slots; -1 marks an empty slot and empty slots follow the occupied ones; every box has one occupied slot or more; an occupied slot names a box of the same block of 256 consecutive boxes or of a block beside it; in every draw some box fills all slots. `far_src_mid`: as for the finest level, with blocks of 32 consecutive boxes. `far_src_top`: as for the finest level, with blocks of 4 consecutive boxes.
All inputs are finite; a program needn't handle non-finite values.
Results may differ from the reference program's by a relative error of at most 0.0003.
Values sent between devices are 32-bit elements; how exact they have to be, the bound alone decides.
A program may use at most 128 MiB of HBM per device.

```python
import jax
import jax.numpy as jnp
from jax import lax

THETA_LOW = 64
PHI_LOW = 128
THETA_MID = 128
PHI_MID = 256
THETA_TOP = 256
PHI_TOP = 512
TOP_DEV = 4
MID_DEV = 32
LOW_DEV = 256
TOP_BOXES = 32
MID_BOXES = 256
LOW_BOXES = 2048
LIST_SLOTS = 8
CLASSES = 16
N_BOX = 8


def far_lists(key, boxes_total, block_size):
    blocks = boxes_total // block_size
    subkeys = jax.random.split(key, 6)
    capacity = jax.random.randint(subkeys[0], (blocks,), 2, LIST_SLOTS + 1)
    busiest = jax.random.randint(subkeys[1], (), 0, blocks)
    capacity = jnp.where(jnp.arange(blocks, dtype=jnp.int32) == busiest, LIST_SLOTS, capacity)
    owners = jnp.arange(boxes_total, dtype=jnp.int32) // block_size
    box_capacity = capacity[owners]
    draws = jax.random.randint(subkeys[2], (boxes_total,), 0, 1 << 20)
    counts = 1 + draws % box_capacity
    counts = jnp.where(jnp.arange(boxes_total, dtype=jnp.int32) == busiest * block_size, LIST_SLOTS, counts)
    offsets = jax.random.randint(subkeys[3], (boxes_total, LIST_SLOTS), -1, 2)
    target = jnp.clip(owners[:, None] + offsets, 0, blocks - 1)
    within = jax.random.randint(subkeys[4], (boxes_total, LIST_SLOTS), 0, block_size)
    sources = target * block_size + within
    occupied = jnp.arange(LIST_SLOTS, dtype=jnp.int32)[None, :] < counts[:, None]
    sources = jnp.where(occupied, sources, -1).astype(jnp.int32)
    classes = jax.random.randint(subkeys[5], (boxes_total, LIST_SLOTS), 0, CLASSES).astype(jnp.int32)
    return (sources, classes)


def draw_far_src_low(key, part):
    return far_lists(jax.random.fold_in(key, 101), LOW_BOXES, LOW_DEV)[0]


def draw_far_class_low(key, part):
    return far_lists(jax.random.fold_in(key, 101), LOW_BOXES, LOW_DEV)[1]


def draw_far_src_mid(key, part):
    return far_lists(jax.random.fold_in(key, 202), MID_BOXES, MID_DEV)[0]


def draw_far_class_mid(key, part):
    return far_lists(jax.random.fold_in(key, 202), MID_BOXES, MID_DEV)[1]


def draw_far_src_top(key, part):
    return far_lists(jax.random.fold_in(key, 303), TOP_BOXES, TOP_DEV)[0]


def draw_far_class_top(key, part):
    return far_lists(jax.random.fold_in(key, 303), TOP_BOXES, TOP_DEV)[1]


def steps_of(stream_key, extent, shards, low, top_value):
    loudness = 1.0
    for dim, parts in shards:
        heights = jax.random.uniform(jax.random.fold_in(jax.random.fold_in(stream_key, 6), dim), (parts,), jnp.float32, low / len(shards), top_value / len(shards))
        loudness = loudness * jnp.repeat(jnp.exp(heights), extent[dim] // parts).reshape((-1,) + (1,) * (len(extent) - 1 - dim))
    return loudness


def scatter_about(own_key, shape, width, bound, pieces=(), held_as=jnp.bfloat16):
    array = jax.random.normal(own_key, shape, jnp.float32) * width
    if len(pieces) > 0:
        array = steps_of(own_key, shape, pieces, -0.22, 0.18) * array
    return jnp.clip(array, min=-bound, max=bound).astype(held_as)


def setup_inputs(seed: int = 0) -> dict:
    keys = jax.random.split(jax.random.key(seed), 11)
    return {
        "low_field": scatter_about(keys[0], (LOW_BOXES, 2, THETA_LOW, PHI_LOW), 1.0, 6.0, ((0, 8), (2, 4)), jnp.float32),
        "far_src_low": draw_far_src_low(jax.random.fold_in(keys[10], 71), 0),
        "far_class_low": draw_far_class_low(jax.random.fold_in(keys[10], 71), 0),
        "table_low": scatter_about(keys[3], (CLASSES, 2, THETA_LOW, PHI_LOW), 0.5, 3.0, ((2, 4),), jnp.float32),
        "far_src_mid": draw_far_src_mid(jax.random.fold_in(keys[10], 71), 0),
        "far_class_mid": draw_far_class_mid(jax.random.fold_in(keys[10], 71), 0),
        "table_mid": scatter_about(keys[6], (CLASSES, 2, THETA_MID, PHI_MID), 0.5, 3.0, ((2, 4),), jnp.float32),
        "far_src_top": draw_far_src_top(jax.random.fold_in(keys[10], 71), 0),
        "far_class_top": draw_far_class_top(jax.random.fold_in(keys[10], 71), 0),
        "table_top": scatter_about(keys[9], (CLASSES, 2, THETA_TOP, PHI_TOP), 0.5, 3.0, ((2, 4),), jnp.float32),
    }


def interp_matrix(samples):
    fine_index = jnp.arange(2 * samples, dtype=jnp.int32)[:, None]
    coarse_index = jnp.arange(samples, dtype=jnp.int32)[None, :]
    offsets = fine_index - 2 * coarse_index
    numerator = jnp.where(offsets % 2 == 0, 0.0, jnp.where(offsets % 4 == 1, 1.0, -1.0)).astype(jnp.float32)
    half_angle = jnp.pi * offsets.astype(jnp.float32) / (2.0 * samples)
    safe_angle = jnp.where(offsets == 0, 1.0, half_angle)
    values = numerator * jnp.cos(safe_angle) / (samples * jnp.sin(safe_angle))
    return jnp.where(offsets == 0, 1.0, values).astype(jnp.float32)


def shift_factors(polar_rows, polar_count, azimuth_count):
    polar = jnp.pi * (polar_rows.astype(jnp.float32) + 0.5) / polar_count
    azimuth = 2.0 * jnp.pi * jnp.arange(azimuth_count, dtype=jnp.int32).astype(jnp.float32) / azimuth_count
    octant = jnp.arange(8, dtype=jnp.int32)
    sign_x = ((octant % 2) * 2 - 1).astype(jnp.float32)[:, None, None]
    sign_y = (((octant // 2) % 2) * 2 - 1).astype(jnp.float32)[:, None, None]
    sign_z = (((octant // 4) % 2) * 2 - 1).astype(jnp.float32)[:, None, None]
    wavenumber = polar_count / 8.0
    sin_polar = jnp.sin(polar)[None, :, None]
    cos_polar = jnp.cos(polar)[None, :, None]
    phases = wavenumber * (sign_x * sin_polar * jnp.cos(azimuth)[None, None, :] + sign_y * sin_polar * jnp.sin(azimuth)[None, None, :] + sign_z * cos_polar)
    return jnp.cos(phases), jnp.sin(phases)


def combine(refined, cosines, sine_part):
    groups = refined.reshape((refined.shape[0] // 8, 8) + refined.shape[1:])
    real_part = jnp.sum(cosines * groups[:, :, 0] - sine_part * groups[:, :, 1], axis=1)
    imag_part = jnp.sum(cosines * groups[:, :, 1] + sine_part * groups[:, :, 0], axis=1)
    return jnp.stack([real_part, imag_part], axis=1)


def slot_term(sources_rows, factor, occupied_col):
    real_part = factor[:, 0] * sources_rows[:, 0] - factor[:, 1] * sources_rows[:, 1]
    imag_part = factor[:, 0] * sources_rows[:, 1] + factor[:, 1] * sources_rows[:, 0]
    stacked = jnp.stack([real_part, imag_part], axis=1)
    return jnp.where(occupied_col[:, None, None, None], stacked, 0.0)


def aggregate_reference(children):
    polar_count = children.shape[2]
    azimuth_count = children.shape[3]
    polar_matrix = interp_matrix(polar_count)
    azimuth_matrix = interp_matrix(azimuth_count)
    cosines, sine_part = shift_factors(jnp.arange(2 * polar_count, dtype=jnp.int32), 2 * polar_count, 2 * azimuth_count)

    def one_block(members):
        half_done = jnp.einsum("ak,bckp->bcap", polar_matrix, members, precision=lax.Precision.HIGHEST)
        refined = jnp.einsum("bcap,qp->bcaq", half_done, azimuth_matrix, precision=lax.Precision.HIGHEST)
        return combine(refined, cosines, sine_part)

    block_size = children.shape[0] // N_BOX
    grouped = children.reshape((N_BOX, block_size) + children.shape[1:])
    parents = lax.map(one_block, grouped)
    return parents.reshape((children.shape[0] // 8,) + parents.shape[2:])


def translate_reference(pattern, far_src, far_class, operator_table):
    block_size = pattern.shape[0] // N_BOX

    def one_block(lists):
        sources, classes = lists
        occupied = sources >= 0
        position = jnp.where(occupied, sources, 0).astype(jnp.int32)
        summed = jnp.zeros((block_size,) + pattern.shape[1:], jnp.float32)
        for slot_index in range(sources.shape[1]):
            sources_rows = jnp.take(pattern, position[:, slot_index], axis=0)
            factor = jnp.take(operator_table, classes[:, slot_index], axis=0)
            summed = summed + slot_term(sources_rows, factor, occupied[:, slot_index])
        return summed

    lists = (far_src.reshape(N_BOX, block_size, -1), far_class.reshape(N_BOX, block_size, -1))
    result = lax.map(one_block, lists)
    return result.reshape(pattern.shape)


def reference(low_field, far_src_low, far_class_low, table_low, far_src_mid, far_class_mid, table_mid, far_src_top, far_class_top, table_top):
    incoming_low = translate_reference(low_field, far_src_low, far_class_low, table_low)
    mid_field = aggregate_reference(low_field)
    incoming_mid = translate_reference(mid_field, far_src_mid, far_class_mid, table_mid)
    top_field = aggregate_reference(mid_field)
    incoming_top = translate_reference(top_field, far_src_top, far_class_top, table_top)
    return (incoming_low, incoming_mid, incoming_top)
```

```python
import functools

import jax
import jax.numpy as jnp
from jax import lax
from jax.experimental import pallas as pl
from jax.experimental.pallas import tpu as pltpu
from jax.sharding import PartitionSpec as P


def interp_entries(rows, columns, samples):
    offsets = rows[:, None] - 2 * columns[None, :]
    numerator = jnp.where(
        offsets % 2 == 0, 0.0, jnp.where(offsets % 4 == 1, 1.0, -1.0)
    ).astype(jnp.float32)
    half_angle = jnp.pi * offsets.astype(jnp.float32) / (2.0 * samples)
    safe_angle = jnp.where(offsets == 0, 1.0, half_angle)
    values = numerator * jnp.cos(safe_angle) / (samples * jnp.sin(safe_angle))
    return jnp.where(offsets == 0, 1.0, values)


def split_bf16(values):
    high = lax.reduce_precision(values, 8, 7)
    return high.astype(jnp.bfloat16), (values - high).astype(jnp.bfloat16)


def iota(count):
    return jnp.arange(count, dtype=jnp.int32)


def aggregate_kernel(
    rows_step, children, polar3, azimuth2, azimuth_low, trig, odd_out, even_out, coeffs, stacked
):
    _, _, depth, width = children.shape
    fine = 2 * width
    odd_rows = polar3.shape[0]
    lanes = 256

    @pl.when(pl.program_id(0) == 0)
    def _():
        for index in range(8):
            bits = (index & 1, index >> 1 & 1, index >> 2 & 1)
            product = trig[bits[0]] * trig[2 + bits[1]] * trig[4 + bits[2]]
            coeffs[index] = -product if sum(bits) >= 2 else product

    parts = [children[i].reshape(2 * depth, width) for i in range(8)]
    for bit in range(3):
        step = 1 << bit
        mixed = list(parts)
        for i in range(8):
            if not i & step:
                mixed[i] = parts[i + step] + parts[i]
                mixed[i + step] = parts[i + step] - parts[i]
        parts = mixed
    for i in range(8):
        high = parts[i].astype(jnp.bfloat16)
        low = (parts[i] - high.astype(jnp.float32)).astype(jnp.bfloat16)
        both = jnp.concatenate([high, low], axis=1)
        wide = jnp.dot(both, azimuth2[...], preferred_element_type=jnp.float32)
        wide += jnp.dot(high, azimuth_low[...], preferred_element_type=jnp.float32)
        wide_high = wide.astype(jnp.bfloat16)
        wide_low = (wide - wide_high.astype(jnp.float32)).astype(jnp.bfloat16)
        for part in range(2):
            rows = slice(part * depth, (part + 1) * depth)
            stacked[i, part] = jnp.concatenate(
                [wide_high[rows], wide_high[rows], wide_low[rows]], axis=0
            )
        factor = coeffs[i, odd_rows : odd_rows + depth, :]
        real, imag = wide[:depth] * factor, wide[depth:] * factor
        odd_count = bin(i).count("1") % 2
        if odd_count:
            real, imag = -imag, real
        if i == 0:
            even_real, even_imag = real, imag
        else:
            even_real, even_imag = even_real + real, even_imag + imag
    even_out[0, 0] = even_real
    even_out[0, 1] = even_imag

    for start in range(0, odd_rows, rows_step):
        rows = slice(start, start + rows_step)
        for lane in range(0, fine, lanes):
            columns = slice(lane, lane + lanes)
            real, imag = None, None
            for i in range(8):
                factor = coeffs[i, rows, columns]
                terms = [
                    jnp.dot(
                        polar3[rows, :],
                        stacked[i, part, :, columns],
                        preferred_element_type=jnp.float32,
                    )
                    * factor
                    for part in range(2)
                ]
                if bin(i).count("1") % 2:
                    terms = [-terms[1], terms[0]]
                real = terms[0] if real is None else real + terms[0]
                imag = terms[1] if imag is None else imag + terms[1]
            for offset in range(0, rows_step, depth):
                owner = (start + offset) // depth
                odd_out[owner, 0, 0, :, columns] = real[offset : offset + depth]
                odd_out[owner, 0, 1, :, columns] = imag[offset : offset + depth]


def aggregate_parts(children, constants):
    boxes, _, depth, width = children.shape
    polar3, azimuth2, azimuth_low, trig = constants
    owners = lax.axis_size("dir")
    parents = boxes // 8
    fine = 2 * width
    odd_rows = owners * depth
    rows_step = min(64, odd_rows)
    whole = lambda array: pl.BlockSpec(array.shape, lambda j: (0,) * array.ndim)
    return pl.pallas_call(
        functools.partial(aggregate_kernel, rows_step),
        grid=(parents,),
        in_specs=[
            pl.BlockSpec((8, 2, depth, width), lambda j: (j, 0, 0, 0)),
            whole(polar3),
            whole(azimuth2),
            whole(azimuth_low),
            whole(trig),
        ],
        out_specs=[
            pl.BlockSpec((owners, 1, 2, depth, fine), lambda j: (0, j, 0, 0, 0)),
            pl.BlockSpec((1, 2, depth, fine), lambda j: (j, 0, 0, 0)),
        ],
        out_shape=[
            jax.ShapeDtypeStruct((owners, parents, 2, depth, fine), jnp.float32),
            jax.ShapeDtypeStruct((parents, 2, depth, fine), jnp.float32),
        ],
        scratch_shapes=[
            pltpu.VMEM((8, odd_rows + depth, fine), jnp.float32),
            pltpu.VMEM((8, 2, 3 * depth, fine), jnp.bfloat16),
        ],
        cost_estimate=pl.CostEstimate(
            flops=boxes * 2 * depth * fine * width * 24,
            bytes_accessed=3 * boxes * 2 * depth * width * 4,
            transcendentals=0,
        ),
        name="aggregate_parts",
    )(children, polar3, azimuth2, azimuth_low, trig)


def aggregate_constants(depth, width):
    owners = lax.axis_size("dir")
    me = lax.axis_index("dir")
    samples = owners * depth
    fine_polar, fine = 2 * samples, 2 * width
    odd = 2 * iota(samples) + 1
    even = 2 * (me * depth + iota(depth))
    polar_high, polar_low = split_bf16(
        interp_entries(odd, me * depth + iota(depth), samples)
    )
    polar3 = jnp.concatenate([polar_high, polar_low, polar_high], axis=1)
    azimuth_high, azimuth_low = split_bf16(interp_entries(iota(fine), iota(width), width).T)
    azimuth2 = jnp.concatenate([azimuth_high, azimuth_high], axis=0)
    rows = jnp.concatenate([odd, even])
    polar = (jnp.pi * (rows.astype(jnp.float32) + 0.5) / fine_polar)[:, None]
    azimuth = (2.0 * jnp.pi * iota(fine).astype(jnp.float32) / fine)[None, :]
    wavenumber = fine_polar / 8.0
    x = wavenumber * (jnp.sin(polar) * jnp.cos(azimuth))
    y = wavenumber * (jnp.sin(polar) * jnp.sin(azimuth))
    z = wavenumber * jnp.cos(polar) + jnp.zeros_like(azimuth)
    trig = jnp.stack([jnp.cos(x), jnp.sin(x), jnp.cos(y), jnp.sin(y), jnp.cos(z), jnp.sin(z)])
    return polar3, azimuth2, azimuth_low, trig


def merge_kernel(received, even, out):
    owners, _, _, depth, fine = received.shape
    for part in range(2):
        total = received[0, 0, part]
        for source in range(1, owners):
            total = total + received[source, 0, part]
        pair = jnp.stack([even[0, part], total], axis=1)
        out[0, part] = pair.reshape(2 * depth, fine)


def merge(received, even):
    owners, parents, _, depth, fine = received.shape
    return pl.pallas_call(
        merge_kernel,
        grid=(parents,),
        in_specs=[
            pl.BlockSpec((owners, 1, 2, depth, fine), lambda j: (0, j, 0, 0, 0)),
            pl.BlockSpec((1, 2, depth, fine), lambda j: (j, 0, 0, 0)),
        ],
        out_specs=pl.BlockSpec((1, 2, 2 * depth, fine), lambda j: (j, 0, 0, 0)),
        out_shape=jax.ShapeDtypeStruct((parents, 2, 2 * depth, fine), jnp.float32),
        cost_estimate=pl.CostEstimate(
            flops=received.size, bytes_accessed=7 * even.size * 4, transcendentals=0
        ),
        name="merge",
    )(received, even)


def aggregate(children, constants):
    odd, even = aggregate_parts(children, constants)
    received = lax.all_to_all(odd, "dir", split_axis=0, concat_axis=0, tiled=True)
    return merge(received, even)


def translate_kernel(
    rows_step, slots, first, src, cls, before, own, after, table, out, sources, factors, sems
):
    block = own.shape[0]
    classes = table.shape[0]
    boxes, _, depth, width = out.shape

    @pl.when(pl.program_id(0) == 0)
    def _():
        copies = [
            pltpu.make_async_copy(before, sources.at[pl.ds(0, block)], sems.at[0]),
            pltpu.make_async_copy(own, sources.at[pl.ds(block, block)], sems.at[1]),
            pltpu.make_async_copy(after, sources.at[pl.ds(2 * block, block)], sems.at[2]),
            pltpu.make_async_copy(table, factors.at[pl.ds(0, classes)], sems.at[3]),
        ]
        for copy in copies:
            copy.start()
        factors[classes] = jnp.zeros(table.shape[1:], jnp.float32)
        for copy in copies:
            copy.wait()

    base = pl.program_id(0) * boxes

    def one_box(box, _):
        picks = []
        for slot in range(slots):
            at = (base + box) * slots + slot
            source = src[at]
            empty = source < 0
            picks.append(
                (
                    jnp.where(empty, block, source - first[0]),
                    jnp.where(empty, classes, cls[at]),
                )
            )
        for row in range(0, depth, rows_step):
            rows = slice(row, row + rows_step)
            real, imag = None, None
            for position, operator in picks:
                p_re = sources[position, 0, rows, :]
                p_im = sources[position, 1, rows, :]
                q_re = factors[operator, 0, rows, :]
                q_im = factors[operator, 1, rows, :]
                new_re = q_re * p_re - q_im * p_im
                new_im = q_re * p_im + q_im * p_re
                real = new_re if real is None else real + new_re
                imag = new_im if imag is None else imag + new_im
            out[box, 0, rows, :] = real
            out[box, 1, rows, :] = imag
        return 0

    lax.fori_loop(0, boxes, one_box, 0)


def translate(before, own, after, far_src, far_class, table):
    block, _, depth, width = own.shape
    slots = far_src.shape[1]
    classes = table.shape[0]
    steps = min(8, block)
    boxes = block // steps
    rows_step = max(8, min(depth, 4096 // width))
    first = jnp.reshape((lax.axis_index("box") - 1) * block, (1,)).astype(jnp.int32)
    hbm = pl.BlockSpec(memory_space=pl.ANY)
    return pl.pallas_call(
        functools.partial(translate_kernel, rows_step, slots),
        grid_spec=pltpu.PrefetchScalarGridSpec(
            num_scalar_prefetch=3,
            grid=(steps,),
            in_specs=[hbm] * 4,
            out_specs=pl.BlockSpec((boxes, 2, depth, width), lambda i, *_: (i, 0, 0, 0)),
            scratch_shapes=[
                pltpu.VMEM((3 * block, 2, depth, width), jnp.float32),
                pltpu.VMEM((classes + 1, 2, depth, width), jnp.float32),
                pltpu.SemaphoreType.DMA((4,)),
            ],
        ),
        out_shape=jax.ShapeDtypeStruct(own.shape, jnp.float32),
        cost_estimate=pl.CostEstimate(
            flops=own.size * slots * 4, bytes_accessed=4 * own.size * 4, transcendentals=0
        ),
        name="translate",
    )(first, far_src.reshape(-1), far_class.reshape(-1), before, own, after, table)


def halo(block):
    size = lax.axis_size("box")
    up = [(i, i + 1) for i in range(size - 1)]
    down = [(j, i) for i, j in up]
    return lax.ppermute(block, "box", up), lax.ppermute(block, "box", down)


def on_device(
    low_field,
    far_src_low,
    far_class_low,
    table_low,
    far_src_mid,
    far_class_mid,
    table_mid,
    far_src_top,
    far_class_top,
    table_top,
):
    depth, width = low_field.shape[2:]
    low_before, low_after = halo(low_field)
    mid_field = aggregate(low_field, aggregate_constants(depth, width))
    mid_before, mid_after = halo(mid_field)
    top_field = aggregate(mid_field, aggregate_constants(2 * depth, 2 * width))
    top_before, top_after = halo(top_field)
    incoming_low = translate(
        low_before, low_field, low_after, far_src_low, far_class_low, table_low
    )
    incoming_mid = translate(
        mid_before, mid_field, mid_after, far_src_mid, far_class_mid, table_mid
    )
    incoming_top = translate(
        top_before, top_field, top_after, far_src_top, far_class_top, table_top
    )
    return (incoming_low, incoming_mid, incoming_top)


def solution(mesh):
    in_specs = (
        P("box", None, "dir", None),
        P("box", None),
        P("box", None),
        P(None, None, "dir", None),
        P("box", None),
        P("box", None),
        P(None, None, "dir", None),
        P("box", None),
        P("box", None),
        P(None, None, "dir", None),
    )
    out_specs = (
        P("box", None, "dir", None),
        P("box", None, "dir", None),
        P("box", None, "dir", None),
    )
    return jax.shard_map(
        on_device, mesh=mesh, in_specs=in_specs, out_specs=out_specs, check_vma=False
    )
```

```python
import functools

import jax
import jax.numpy as jnp
from jax import lax
from jax.experimental import pallas as pl
from jax.experimental.pallas import tpu as pltpu
from jax.sharding import PartitionSpec as P


def interp_entries(rows, columns, samples):
    offsets = rows[:, None] - 2 * columns[None, :]
    numerator = jnp.where(
        offsets % 2 == 0, 0.0, jnp.where(offsets % 4 == 1, 1.0, -1.0)
    ).astype(jnp.float32)
    half_angle = jnp.pi * offsets.astype(jnp.float32) / (2.0 * samples)
    safe_angle = jnp.where(offsets == 0, 1.0, half_angle)
    values = numerator * jnp.cos(safe_angle) / (samples * jnp.sin(safe_angle))
    return jnp.where(offsets == 0, 1.0, values)


def split_bf16(values):
    high = lax.reduce_precision(values, 8, 7)
    return high.astype(jnp.bfloat16), (values - high).astype(jnp.bfloat16)


def iota(count):
    return jnp.arange(count, dtype=jnp.int32)


def aggregate_kernel(
    rows_step, children, polar3, azimuth2, azimuth_low, trig, *outs_and_scratch
):
    *odd_outs, even_out, coeffs, stacked = outs_and_scratch
    parents = even_out.shape[0]
    _, _, depth, width = children.shape
    fine = 2 * width
    odd_rows = polar3.shape[0]
    lanes = 256

    @pl.when(pl.program_id(0) == 0)
    def _():
        for index in range(8):
            bits = (index & 1, index >> 1 & 1, index >> 2 & 1)
            product = trig[bits[0]] * trig[2 + bits[1]] * trig[4 + bits[2]]
            coeffs[index] = -product if sum(bits) >= 2 else product

    def one_parent(parent, _):
        parts = [children[8 * parent + i].reshape(2 * depth, width) for i in range(8)]
        for bit in range(3):
            step = 1 << bit
            mixed = list(parts)
            for i in range(8):
                if not i & step:
                    mixed[i] = parts[i + step] + parts[i]
                    mixed[i + step] = parts[i + step] - parts[i]
            parts = mixed
        for i in range(8):
            high = parts[i].astype(jnp.bfloat16)
            low = (parts[i] - high.astype(jnp.float32)).astype(jnp.bfloat16)
            both = jnp.concatenate([high, low], axis=1)
            wide = jnp.dot(both, azimuth2[...], preferred_element_type=jnp.float32)
            wide += jnp.dot(high, azimuth_low[...], preferred_element_type=jnp.float32)
            wide_high = wide.astype(jnp.bfloat16)
            wide_low = (wide - wide_high.astype(jnp.float32)).astype(jnp.bfloat16)
            for part in range(2):
                rows = slice(part * depth, (part + 1) * depth)
                stacked[i, part] = jnp.concatenate(
                    [wide_high[rows], wide_high[rows], wide_low[rows]], axis=0
                )
            factor = coeffs[i, odd_rows : odd_rows + depth, :]
            real, imag = wide[:depth] * factor, wide[depth:] * factor
            if bin(i).count("1") % 2:
                real, imag = -imag, real
            if i == 0:
                even_real, even_imag = real, imag
            else:
                even_real, even_imag = even_real + real, even_imag + imag
        even_out[parent, 0] = even_real
        even_out[parent, 1] = even_imag

        for start in range(0, odd_rows, rows_step):
            rows = slice(start, start + rows_step)
            for lane in range(0, fine, lanes):
                columns = slice(lane, lane + lanes)
                real, imag = None, None
                for i in range(8):
                    factor = coeffs[i, rows, columns]
                    terms = [
                        jnp.dot(
                            polar3[rows, :],
                            stacked[i, part, :, columns],
                            preferred_element_type=jnp.float32,
                        )
                        * factor
                        for part in range(2)
                    ]
                    if bin(i).count("1") % 2:
                        terms = [-terms[1], terms[0]]
                    real = terms[0] if real is None else real + terms[0]
                    imag = terms[1] if imag is None else imag + terms[1]
                for offset in range(0, rows_step, depth):
                    owner = (start + offset) // depth
                    odd_outs[owner][parent, 0, :, columns] = real[offset : offset + depth]
                    odd_outs[owner][parent, 1, :, columns] = imag[offset : offset + depth]
        return 0

    if parents == 1:
        one_parent(0, 0)
    else:
        lax.fori_loop(0, parents, one_parent, 0)


def aggregate_parts(children, constants):
    boxes, _, depth, width = children.shape
    polar3, azimuth2, azimuth_low, trig = constants
    owners = lax.axis_size("dir")
    parents = boxes // 8
    group = max(1, parents // 8)
    fine = 2 * width
    odd_rows = owners * depth
    rows_step = min(64, odd_rows)
    whole = lambda array: pl.BlockSpec(array.shape, lambda j: (0,) * array.ndim)
    return pl.pallas_call(
        functools.partial(aggregate_kernel, rows_step),
        grid=(parents // group,),
        in_specs=[
            pl.BlockSpec((8 * group, 2, depth, width), lambda j: (j, 0, 0, 0)),
            whole(polar3),
            whole(azimuth2),
            whole(azimuth_low),
            whole(trig),
        ],
        out_specs=[pl.BlockSpec((group, 2, depth, fine), lambda j: (j, 0, 0, 0))]
        * (owners + 1),
        out_shape=[jax.ShapeDtypeStruct((parents, 2, depth, fine), jnp.float32)]
        * (owners + 1),
        scratch_shapes=[
            pltpu.VMEM((8, odd_rows + depth, fine), jnp.float32),
            pltpu.VMEM((8, 2, 3 * depth, fine), jnp.bfloat16),
        ],
        cost_estimate=pl.CostEstimate(
            flops=boxes * 2 * depth * fine * width * 24,
            bytes_accessed=3 * boxes * 2 * depth * width * 4,
            transcendentals=0,
        ),
        name="aggregate_parts",
    )(children, polar3, azimuth2, azimuth_low, trig)


def aggregate_constants(depth, width):
    owners = lax.axis_size("dir")
    me = lax.axis_index("dir")
    samples = owners * depth
    fine_polar, fine = 2 * samples, 2 * width
    mine = me * depth
    odd = 2 * ((iota(samples) + mine) % samples) + 1
    even = 2 * (mine + iota(depth))
    polar_high, polar_low = split_bf16(interp_entries(odd, mine + iota(depth), samples))
    polar3 = jnp.concatenate([polar_high, polar_low, polar_high], axis=1)
    azimuth_high, azimuth_low = split_bf16(interp_entries(iota(fine), iota(width), width).T)
    azimuth2 = jnp.concatenate([azimuth_high, azimuth_high], axis=0)
    rows = jnp.concatenate([odd, even])
    polar = (jnp.pi * (rows.astype(jnp.float32) + 0.5) / fine_polar)[:, None]
    azimuth = (2.0 * jnp.pi * iota(fine).astype(jnp.float32) / fine)[None, :]
    wavenumber = fine_polar / 8.0
    x = wavenumber * (jnp.sin(polar) * jnp.cos(azimuth))
    y = wavenumber * (jnp.sin(polar) * jnp.sin(azimuth))
    z = wavenumber * jnp.cos(polar) + jnp.zeros_like(azimuth)
    trig = jnp.stack([jnp.cos(x), jnp.sin(x), jnp.cos(y), jnp.sin(y), jnp.cos(z), jnp.sin(z)])
    return polar3, azimuth2, azimuth_low, trig


def merge_kernel(count, *refs):
    even, terms, out, tiles = refs[0], refs[1 : 1 + count], refs[-2], refs[-1]
    parents, _, depth, fine = even.shape
    for parent in range(parents):
        for part in range(2):
            for lane in range(0, fine, 128):
                columns = slice(lane, lane + 128)
                total = terms[0][parent, part, :, columns]
                for term in terms[1:]:
                    total = total + term[parent, part, :, columns]
                tile = tiles.at[(parent * 2 + part) * (fine // 128) + lane // 128]
                tile[pl.ds(0, depth, stride=2), :] = even[parent, part, :, columns]
                tile[pl.ds(1, depth, stride=2), :] = total
                out[parent, part, :, columns] = tile[...]


def merge(even, terms, after):
    parents, _, depth, fine = even.shape
    group = max(1, parents // 4)
    piece = pl.BlockSpec((group, 2, depth, fine), lambda j: (j, 0, 0, 0))
    return pl.pallas_call(
        functools.partial(merge_kernel, len(terms)),
        grid=(parents // group,),
        in_specs=[piece] * (1 + len(terms)) + [pl.BlockSpec(memory_space=pl.ANY)] * len(after),
        out_specs=pl.BlockSpec((group, 2, 2 * depth, fine), lambda j: (j, 0, 0, 0)),
        out_shape=jax.ShapeDtypeStruct((parents, 2, 2 * depth, fine), jnp.float32),
        scratch_shapes=[pltpu.VMEM((group * 2 * (fine // 128), 2 * depth, 128), jnp.float32)],
        cost_estimate=pl.CostEstimate(
            flops=even.size * len(terms), bytes_accessed=7 * even.size * 4, transcendentals=0
        ),
        name="merge",
    )(even, *terms, *after)


def exchange(odd):
    owners = len(odd)
    if owners != 4:
        send = jnp.stack(odd)
        send = jnp.roll(send, lax.axis_index("dir"), axis=0)
        received = lax.all_to_all(send, "dir", split_axis=0, concat_axis=0, tiled=True)
        return [received[i] for i in range(owners)]
    own, following, opposite, preceding = odd
    from_first = lax.ppermute(preceding, "dir", [(0, 1)])
    from_last = lax.ppermute(following, "dir", [(3, 2)])
    up = lax.ppermute(following, "dir", [(0, 1), (1, 2), (2, 3)])
    down = lax.ppermute(preceding, "dir", [(1, 0), (2, 1), (3, 2)])
    outer = lax.ppermute(opposite, "dir", [(0, 2), (3, 1)])
    passed_on = opposite + (from_first + from_last)
    inner = lax.ppermute(passed_on, "dir", [(1, 3), (2, 0)])
    return [own, up, down, outer, inner]


def translate_kernel(
    rows_step, slots, first, src, cls, before, own, after, table, out, sources, factors, sems
):
    block = own.shape[0]
    classes = table.shape[0]
    boxes, _, depth, width = out.shape

    @pl.when(pl.program_id(0) == 0)
    def _():
        copies = [
            pltpu.make_async_copy(before, sources.at[pl.ds(0, block)], sems.at[0]),
            pltpu.make_async_copy(own, sources.at[pl.ds(block, block)], sems.at[1]),
            pltpu.make_async_copy(after, sources.at[pl.ds(2 * block, block)], sems.at[2]),
            pltpu.make_async_copy(table, factors.at[pl.ds(0, classes)], sems.at[3]),
        ]
        for copy in copies:
            copy.start()
        factors[classes] = jnp.zeros(table.shape[1:], jnp.float32)
        for copy in copies:
            copy.wait()

    base = pl.program_id(0) * boxes

    def one_box(box, _):
        picks = []
        for slot in range(slots):
            at = (base + box) * slots + slot
            source = src[at]
            empty = source < 0
            picks.append(
                (
                    jnp.where(empty, block, source - first[0]),
                    jnp.where(empty, classes, cls[at]),
                )
            )
        for row in range(0, depth, rows_step):
            rows = slice(row, row + rows_step)
            real, imag = None, None
            for position, operator in picks:
                p_re = sources[position, 0, rows, :]
                p_im = sources[position, 1, rows, :]
                q_re = factors[operator, 0, rows, :]
                q_im = factors[operator, 1, rows, :]
                new_re = q_re * p_re - q_im * p_im
                new_im = q_re * p_im + q_im * p_re
                real = new_re if real is None else real + new_re
                imag = new_im if imag is None else imag + new_im
            out[box, 0, rows, :] = real
            out[box, 1, rows, :] = imag
        return 0

    lax.fori_loop(0, boxes, one_box, 0)


def translate(before, own, after, far_src, far_class, table):
    block, _, depth, width = own.shape
    slots = far_src.shape[1]
    classes = table.shape[0]
    steps = min(8, block)
    boxes = block // steps
    rows_step = max(8, min(depth, 4096 // width))
    first = jnp.reshape((lax.axis_index("box") - 1) * block, (1,)).astype(jnp.int32)
    hbm = pl.BlockSpec(memory_space=pl.ANY)
    return pl.pallas_call(
        functools.partial(translate_kernel, rows_step, slots),
        grid_spec=pltpu.PrefetchScalarGridSpec(
            num_scalar_prefetch=3,
            grid=(steps,),
            in_specs=[hbm] * 4,
            out_specs=pl.BlockSpec((boxes, 2, depth, width), lambda i, *_: (i, 0, 0, 0)),
            scratch_shapes=[
                pltpu.VMEM((3 * block, 2, depth, width), jnp.float32),
                pltpu.VMEM((classes + 1, 2, depth, width), jnp.float32),
                pltpu.SemaphoreType.DMA((4,)),
            ],
        ),
        out_shape=jax.ShapeDtypeStruct(own.shape, jnp.float32),
        cost_estimate=pl.CostEstimate(
            flops=own.size * slots * 4, bytes_accessed=4 * own.size * 4, transcendentals=0
        ),
        name="translate",
    )(first, far_src.reshape(-1), far_class.reshape(-1), before, own, after, table)


def halo(block):
    size = lax.axis_size("box")
    up = [(i, i + 1) for i in range(size - 1)]
    down = [(j, i) for i, j in up]
    return lax.ppermute(block, "box", up), lax.ppermute(block, "box", down)


def on_device(
    low_field,
    far_src_low,
    far_class_low,
    table_low,
    far_src_mid,
    far_class_mid,
    table_mid,
    far_src_top,
    far_class_top,
    table_top,
):
    depth, width = low_field.shape[2:]
    low_before, low_after = halo(low_field)
    low_odd = aggregate_parts(low_field, aggregate_constants(depth, width))
    mid_field = merge(low_odd[-1], exchange(low_odd[:-1]), ())
    mid_before, mid_after = halo(mid_field)
    mid_odd = aggregate_parts(mid_field, aggregate_constants(2 * depth, 2 * width))
    incoming_low = translate(
        low_before, low_field, low_after, far_src_low, far_class_low, table_low
    )
    top_field = merge(mid_odd[-1], exchange(mid_odd[:-1]), (incoming_low,))
    top_before, top_after = halo(top_field)
    incoming_mid = translate(
        mid_before, mid_field, mid_after, far_src_mid, far_class_mid, table_mid
    )
    incoming_top = translate(
        top_before, top_field, top_after, far_src_top, far_class_top, table_top
    )
    return (incoming_low, incoming_mid, incoming_top)


def solution(mesh):
    in_specs = (
        P("box", None, "dir", None),
        P("box", None),
        P("box", None),
        P(None, None, "dir", None),
        P("box", None),
        P("box", None),
        P(None, None, "dir", None),
        P("box", None),
        P("box", None),
        P(None, None, "dir", None),
    )
    out_specs = (
        P("box", None, "dir", None),
        P("box", None, "dir", None),
        P("box", None, "dir", None),
    )
    return jax.shard_map(
        on_device, mesh=mesh, in_specs=in_specs, out_specs=out_specs, check_vma=False
    )
```

```python
import functools

import jax
import jax.numpy as jnp
from jax import lax
from jax.experimental import pallas as pl
from jax.experimental.pallas import tpu as pltpu
from jax.sharding import PartitionSpec as P


def interp_entries(rows, columns, samples):
    offsets = rows[:, None] - 2 * columns[None, :]
    numerator = jnp.where(
        offsets % 2 == 0, 0.0, jnp.where(offsets % 4 == 1, 1.0, -1.0)
    ).astype(jnp.float32)
    half_angle = jnp.pi * offsets.astype(jnp.float32) / (2.0 * samples)
    safe_angle = jnp.where(offsets == 0, 1.0, half_angle)
    values = numerator * jnp.cos(safe_angle) / (samples * jnp.sin(safe_angle))
    return jnp.where(offsets == 0, 1.0, values)


def split_bf16(values):
    high = lax.reduce_precision(values, 8, 7)
    return high.astype(jnp.bfloat16), (values - high).astype(jnp.bfloat16)


def iota(count):
    return jnp.arange(count, dtype=jnp.int32)


def aggregate_kernel(
    rows_step, children, polar3, azimuth2, azimuth_low, trig, *outs_and_scratch
):
    *odd_outs, even_out, coeffs, stacked = outs_and_scratch
    parents = even_out.shape[0]
    _, _, depth, width = children.shape
    fine = 2 * width
    odd_rows = polar3.shape[0]
    lanes = 256

    @pl.when(pl.program_id(0) == 0)
    def _():
        for index in range(8):
            bits = (index & 1, index >> 1 & 1, index >> 2 & 1)
            product = trig[bits[0]] * trig[2 + bits[1]] * trig[4 + bits[2]]
            coeffs[index] = -product if sum(bits) >= 2 else product

    def one_parent(parent, _):
        parts = [children[8 * parent + i].reshape(2 * depth, width) for i in range(8)]
        for bit in range(3):
            step = 1 << bit
            mixed = list(parts)
            for i in range(8):
                if not i & step:
                    mixed[i] = parts[i + step] + parts[i]
                    mixed[i + step] = parts[i + step] - parts[i]
            parts = mixed
        for i in range(8):
            high = parts[i].astype(jnp.bfloat16)
            low = (parts[i] - high.astype(jnp.float32)).astype(jnp.bfloat16)
            both = jnp.concatenate([high, low], axis=1)
            wide = jnp.dot(both, azimuth2[...], preferred_element_type=jnp.float32)
            wide += jnp.dot(high, azimuth_low[...], preferred_element_type=jnp.float32)
            wide_high = wide.astype(jnp.bfloat16)
            wide_low = (wide - wide_high.astype(jnp.float32)).astype(jnp.bfloat16)
            for part in range(2):
                rows = slice(part * depth, (part + 1) * depth)
                stacked[i, part] = jnp.concatenate(
                    [wide_high[rows], wide_high[rows], wide_low[rows]], axis=0
                )
            factor = coeffs[i, odd_rows : odd_rows + depth, :]
            real, imag = wide[:depth] * factor, wide[depth:] * factor
            if bin(i).count("1") % 2:
                real, imag = -imag, real
            if i == 0:
                even_real, even_imag = real, imag
            else:
                even_real, even_imag = even_real + real, even_imag + imag
        even_out[parent, 0] = even_real
        even_out[parent, 1] = even_imag

        for start in range(0, odd_rows, rows_step):
            rows = slice(start, start + rows_step)
            for lane in range(0, fine, lanes):
                columns = slice(lane, lane + lanes)
                real, imag = None, None
                for i in range(8):
                    factor = coeffs[i, rows, columns]
                    terms = [
                        jnp.dot(
                            polar3[rows, :],
                            stacked[i, part, :, columns],
                            preferred_element_type=jnp.float32,
                        )
                        * factor
                        for part in range(2)
                    ]
                    if bin(i).count("1") % 2:
                        terms = [-terms[1], terms[0]]
                    real = terms[0] if real is None else real + terms[0]
                    imag = terms[1] if imag is None else imag + terms[1]
                for offset in range(0, rows_step, depth):
                    owner = (start + offset) // depth
                    odd_outs[owner][parent, 0, :, columns] = real[offset : offset + depth]
                    odd_outs[owner][parent, 1, :, columns] = imag[offset : offset + depth]
        return 0

    if parents == 1:
        one_parent(0, 0)
    else:
        lax.fori_loop(0, parents, one_parent, 0)


def aggregate_parts(children, constants, half, halves):
    boxes, _, depth, width = children.shape
    boxes //= halves
    polar3, azimuth2, azimuth_low, trig = constants
    owners = lax.axis_size("dir")
    parents = boxes // 8
    group = max(1, parents // 8)
    steps = parents // group
    fine = 2 * width
    odd_rows = owners * depth
    rows_step = min(64, odd_rows)
    whole = lambda array: pl.BlockSpec(array.shape, lambda j: (0,) * array.ndim)
    return pl.pallas_call(
        functools.partial(aggregate_kernel, rows_step),
        grid=(steps,),
        in_specs=[
            pl.BlockSpec((8 * group, 2, depth, width), lambda j: (j + half * steps, 0, 0, 0)),
            whole(polar3),
            whole(azimuth2),
            whole(azimuth_low),
            whole(trig),
        ],
        out_specs=[pl.BlockSpec((group, 2, depth, fine), lambda j: (j, 0, 0, 0))]
        * (owners + 1),
        out_shape=[jax.ShapeDtypeStruct((parents, 2, depth, fine), jnp.float32)]
        * (owners + 1),
        scratch_shapes=[
            pltpu.VMEM((8, odd_rows + depth, fine), jnp.float32),
            pltpu.VMEM((8, 2, 3 * depth, fine), jnp.bfloat16),
        ],
        cost_estimate=pl.CostEstimate(
            flops=boxes * 2 * depth * fine * width * 24,
            bytes_accessed=3 * boxes * 2 * depth * width * 4,
            transcendentals=0,
        ),
        name="aggregate_parts",
    )(children, polar3, azimuth2, azimuth_low, trig)


def aggregate_constants(depth, width):
    owners = lax.axis_size("dir")
    me = lax.axis_index("dir")
    samples = owners * depth
    fine_polar, fine = 2 * samples, 2 * width
    mine = me * depth
    odd = 2 * ((iota(samples) + mine) % samples) + 1
    even = 2 * (mine + iota(depth))
    polar_high, polar_low = split_bf16(interp_entries(odd, mine + iota(depth), samples))
    polar3 = jnp.concatenate([polar_high, polar_low, polar_high], axis=1)
    azimuth_high, azimuth_low = split_bf16(interp_entries(iota(fine), iota(width), width).T)
    azimuth2 = jnp.concatenate([azimuth_high, azimuth_high], axis=0)
    rows = jnp.concatenate([odd, even])
    polar = (jnp.pi * (rows.astype(jnp.float32) + 0.5) / fine_polar)[:, None]
    azimuth = (2.0 * jnp.pi * iota(fine).astype(jnp.float32) / fine)[None, :]
    wavenumber = fine_polar / 8.0
    x = wavenumber * (jnp.sin(polar) * jnp.cos(azimuth))
    y = wavenumber * (jnp.sin(polar) * jnp.sin(azimuth))
    z = wavenumber * jnp.cos(polar) + jnp.zeros_like(azimuth)
    trig = jnp.stack([jnp.cos(x), jnp.sin(x), jnp.cos(y), jnp.sin(y), jnp.cos(z), jnp.sin(z)])
    return polar3, azimuth2, azimuth_low, trig


def merge_kernel(count, *refs):
    even, terms, out, tiles = refs[0], refs[1 : 1 + count], refs[-2], refs[-1]
    parents, _, depth, fine = even.shape
    for parent in range(parents):
        for part in range(2):
            for lane in range(0, fine, 128):
                columns = slice(lane, lane + 128)
                total = terms[0][parent, part, :, columns]
                for term in terms[1:]:
                    total = total + term[parent, part, :, columns]
                tile = tiles.at[(parent * 2 + part) * (fine // 128) + lane // 128]
                tile[pl.ds(0, depth, stride=2), :] = even[parent, part, :, columns]
                tile[pl.ds(1, depth, stride=2), :] = total
                out[parent, part, :, columns] = tile[...]


def merge(even, terms, after):
    parents, _, depth, fine = even.shape
    group = max(1, parents // 4)
    piece = pl.BlockSpec((group, 2, depth, fine), lambda j: (j, 0, 0, 0))
    return pl.pallas_call(
        functools.partial(merge_kernel, len(terms)),
        grid=(parents // group,),
        in_specs=[piece] * (1 + len(terms)) + [pl.BlockSpec(memory_space=pl.ANY)] * len(after),
        out_specs=pl.BlockSpec((group, 2, 2 * depth, fine), lambda j: (j, 0, 0, 0)),
        out_shape=jax.ShapeDtypeStruct((parents, 2, 2 * depth, fine), jnp.float32),
        scratch_shapes=[pltpu.VMEM((group * 2 * (fine // 128), 2 * depth, 128), jnp.float32)],
        cost_estimate=pl.CostEstimate(
            flops=even.size * len(terms), bytes_accessed=7 * even.size * 4, transcendentals=0
        ),
        name="merge",
    )(even, *terms, *after)


def exchange(odd):
    owners = len(odd)
    if owners != 4:
        send = jnp.stack(odd)
        send = jnp.roll(send, lax.axis_index("dir"), axis=0)
        received = lax.all_to_all(send, "dir", split_axis=0, concat_axis=0, tiled=True)
        return [received[i] for i in range(owners)]
    own, following, opposite, preceding = odd
    from_first = lax.ppermute(preceding, "dir", [(0, 1)])
    from_last = lax.ppermute(following, "dir", [(3, 2)])
    up = lax.ppermute(following, "dir", [(0, 1), (1, 2), (2, 3)])
    down = lax.ppermute(preceding, "dir", [(1, 0), (2, 1), (3, 2)])
    outer = lax.ppermute(opposite, "dir", [(0, 2), (3, 1)])
    passed_on = opposite + (from_first + from_last)
    inner = lax.ppermute(passed_on, "dir", [(1, 3), (2, 0)])
    return [own, up, down, outer, inner]


def translate_kernel(
    rows_step, slots, first, src, cls, *refs
):
    *pieces, table, out, sources, factors, sems = refs
    block = sources.shape[0] // 3
    classes = table.shape[0]
    boxes, _, depth, _ = out.shape

    @pl.when(pl.program_id(0) == 0)
    def _():
        copies = [pltpu.make_async_copy(table, factors.at[pl.ds(0, classes)], sems.at[0])]
        at = 0
        for index, piece in enumerate(pieces):
            size = piece.shape[0]
            target = sources.at[pl.ds(at, size)]
            copies.append(pltpu.make_async_copy(piece, target, sems.at[1 + index]))
            at += size
        for copy in copies:
            copy.start()
        factors[classes] = jnp.zeros(table.shape[1:], jnp.float32)
        for copy in copies:
            copy.wait()

    base = pl.program_id(0) * boxes

    def one_box(box, _):
        picks = []
        for slot in range(slots):
            at = (base + box) * slots + slot
            source = src[at]
            empty = source < 0
            picks.append(
                (
                    jnp.where(empty, block, source - first[0]),
                    jnp.where(empty, classes, cls[at]),
                )
            )
        for row in range(0, depth, rows_step):
            rows = slice(row, row + rows_step)
            real, imag = None, None
            for position, operator in picks:
                p_re = sources[position, 0, rows, :]
                p_im = sources[position, 1, rows, :]
                q_re = factors[operator, 0, rows, :]
                q_im = factors[operator, 1, rows, :]
                new_re = q_re * p_re - q_im * p_im
                new_im = q_re * p_im + q_im * p_re
                real = new_re if real is None else real + new_re
                imag = new_im if imag is None else imag + new_im
            out[box, 0, rows, :] = real
            out[box, 1, rows, :] = imag
        return 0

    lax.fori_loop(0, boxes, one_box, 0)


def translate(before, own, after, far_src, far_class, table):
    pieces = [*before, *own, *after]
    block = sum(piece.shape[0] for piece in own)
    _, _, depth, width = own[0].shape
    size = 2 * block * depth * width
    slots = far_src.shape[1]
    classes = table.shape[0]
    steps = min(8, block)
    boxes = block // steps
    rows_step = max(8, min(depth, 4096 // width))
    first = jnp.reshape((lax.axis_index("box") - 1) * block, (1,)).astype(jnp.int32)
    hbm = pl.BlockSpec(memory_space=pl.ANY)
    return pl.pallas_call(
        functools.partial(translate_kernel, rows_step, slots),
        grid_spec=pltpu.PrefetchScalarGridSpec(
            num_scalar_prefetch=3,
            grid=(steps,),
            in_specs=[hbm] * (len(pieces) + 1),
            out_specs=pl.BlockSpec((boxes, 2, depth, width), lambda i, *_: (i, 0, 0, 0)),
            scratch_shapes=[
                pltpu.VMEM((3 * block, 2, depth, width), jnp.float32),
                pltpu.VMEM((classes + 1, 2, depth, width), jnp.float32),
                pltpu.SemaphoreType.DMA((len(pieces) + 1,)),
            ],
        ),
        out_shape=jax.ShapeDtypeStruct((block, 2, depth, width), jnp.float32),
        cost_estimate=pl.CostEstimate(
            flops=size * slots * 4, bytes_accessed=4 * size * 4, transcendentals=0
        ),
        name="translate",
    )(first, far_src.reshape(-1), far_class.reshape(-1), *pieces, table)


def halo(block):
    size = lax.axis_size("box")
    up = [(i, i + 1) for i in range(size - 1)]
    down = [(j, i) for i, j in up]
    before = lax.ppermute(block, "box", up)
    after = lax.ppermute(block, "box", down)
    return before, after


def on_device(
    low_field,
    far_src_low,
    far_class_low,
    table_low,
    far_src_mid,
    far_class_mid,
    table_mid,
    far_src_top,
    far_class_top,
    table_top,
):
    depth, width = low_field.shape[2:]
    halves = 2 if low_field.shape[0] // 64 % 2 == 0 else 1
    low_constants = aggregate_constants(depth, width)
    mid_constants = aggregate_constants(2 * depth, 2 * width)
    low_parts = []
    for half in range(halves):
        odd = aggregate_parts(low_field, low_constants, half, halves)
        low_parts.append((odd[-1], exchange(odd[:-1])))
    low_before, low_after = halo(low_field)
    mid_field, mid_halos, mid_parts = [], [], []
    for half in range(halves):
        mid = merge(*low_parts[half], ())
        mid_field.append(mid)
        odd = aggregate_parts(mid, mid_constants, 0, 1)
        mid_parts.append((odd[-1], exchange(odd[:-1])))
        mid_halos.append(halo(mid))
    incoming_low = translate(
        [low_before], [low_field], [low_after], far_src_low, far_class_low, table_low
    )
    top_field, top_halos = [], []
    for half in range(halves):
        after = (incoming_low,) if half == halves - 1 else ()
        top = merge(*mid_parts[half], after)
        top_field.append(top)
        top_halos.append(halo(top))
    mid_before, mid_after = zip(*mid_halos)
    incoming_mid = translate(
        mid_before, mid_field, mid_after, far_src_mid, far_class_mid, table_mid
    )
    top_before, top_after = zip(*top_halos)
    incoming_top = translate(
        top_before, top_field, top_after, far_src_top, far_class_top, table_top
    )
    return (incoming_low, incoming_mid, incoming_top)


def solution(mesh):
    in_specs = (
        P("box", None, "dir", None),
        P("box", None),
        P("box", None),
        P(None, None, "dir", None),
        P("box", None),
        P("box", None),
        P(None, None, "dir", None),
        P("box", None),
        P("box", None),
        P(None, None, "dir", None),
    )
    out_specs = (
        P("box", None, "dir", None),
        P("box", None, "dir", None),
        P("box", None, "dir", None),
    )
    return jax.shard_map(
        on_device, mesh=mesh, in_specs=in_specs, out_specs=out_specs, check_vma=False
    )
```

```python
import functools

import jax
import jax.numpy as jnp
from jax import lax
from jax.experimental import pallas as pl
from jax.experimental.pallas import tpu as pltpu
from jax.sharding import PartitionSpec as P


def interp_entries(rows, columns, samples):
    offsets = rows[:, None] - 2 * columns[None, :]
    numerator = jnp.where(
        offsets % 2 == 0, 0.0, jnp.where(offsets % 4 == 1, 1.0, -1.0)
    ).astype(jnp.float32)
    half_angle = jnp.pi * offsets.astype(jnp.float32) / (2.0 * samples)
    safe_angle = jnp.where(offsets == 0, 1.0, half_angle)
    values = numerator * jnp.cos(safe_angle) / (samples * jnp.sin(safe_angle))
    return jnp.where(offsets == 0, 1.0, values)


def split_bf16(values):
    high = lax.reduce_precision(values, 8, 7)
    return high.astype(jnp.bfloat16), (values - high).astype(jnp.bfloat16)


def iota(count):
    return jnp.arange(count, dtype=jnp.int32)


def aggregate_kernel(
    rows_step, children, polar3, azimuth2, azimuth_low, trig, *outs_and_scratch
):
    *odd_outs, even_out, coeffs, stacked = outs_and_scratch
    parents = even_out.shape[0]
    _, _, depth, width = children.shape
    fine = 2 * width
    odd_rows = polar3.shape[0]
    lanes = 256

    @pl.when(pl.program_id(0) == 0)
    def _():
        for index in range(8):
            bits = (index & 1, index >> 1 & 1, index >> 2 & 1)
            product = trig[bits[0]] * trig[2 + bits[1]] * trig[4 + bits[2]]
            coeffs[index] = -product if sum(bits) >= 2 else product

    def one_parent(parent, _):
        parts = [children[8 * parent + i].reshape(2 * depth, width) for i in range(8)]
        for bit in range(3):
            step = 1 << bit
            mixed = list(parts)
            for i in range(8):
                if not i & step:
                    mixed[i] = parts[i + step] + parts[i]
                    mixed[i + step] = parts[i + step] - parts[i]
            parts = mixed
        for i in range(8):
            high = parts[i].astype(jnp.bfloat16)
            low = (parts[i] - high.astype(jnp.float32)).astype(jnp.bfloat16)
            both = jnp.concatenate([high, low], axis=1)
            wide = jnp.dot(both, azimuth2[...], preferred_element_type=jnp.float32)
            wide += jnp.dot(high, azimuth_low[...], preferred_element_type=jnp.float32)
            wide_high = wide.astype(jnp.bfloat16)
            wide_low = (wide - wide_high.astype(jnp.float32)).astype(jnp.bfloat16)
            for part in range(2):
                rows = slice(part * depth, (part + 1) * depth)
                stacked[i, part] = jnp.concatenate(
                    [wide_high[rows], wide_high[rows], wide_low[rows]], axis=0
                )
            factor = coeffs[i, odd_rows : odd_rows + depth, :]
            real, imag = wide[:depth] * factor, wide[depth:] * factor
            if bin(i).count("1") % 2:
                real, imag = -imag, real
            if i == 0:
                even_real, even_imag = real, imag
            else:
                even_real, even_imag = even_real + real, even_imag + imag
        even_out[parent, 0] = even_real
        even_out[parent, 1] = even_imag

        for start in range(0, odd_rows, rows_step):
            rows = slice(start, start + rows_step)
            for lane in range(0, fine, lanes):
                columns = slice(lane, lane + lanes)
                real, imag = None, None
                for i in range(8):
                    factor = coeffs[i, rows, columns]
                    terms = [
                        jnp.dot(
                            polar3[rows, :],
                            stacked[i, part, :, columns],
                            preferred_element_type=jnp.float32,
                        )
                        * factor
                        for part in range(2)
                    ]
                    if bin(i).count("1") % 2:
                        terms = [-terms[1], terms[0]]
                    real = terms[0] if real is None else real + terms[0]
                    imag = terms[1] if imag is None else imag + terms[1]
                for offset in range(0, rows_step, depth):
                    owner = (start + offset) // depth
                    odd_outs[owner][parent, 0, :, columns] = real[offset : offset + depth]
                    odd_outs[owner][parent, 1, :, columns] = imag[offset : offset + depth]
        return 0

    if parents == 1:
        one_parent(0, 0)
    else:
        lax.fori_loop(0, parents, one_parent, 0)


def aggregate_parts(children, constants):
    boxes, _, depth, width = children.shape
    polar3, azimuth2, azimuth_low, trig = constants
    owners = lax.axis_size("dir")
    parents = boxes // 8
    group = max(1, parents // 8)
    fine = 2 * width
    odd_rows = owners * depth
    rows_step = min(64, odd_rows)
    whole = lambda array: pl.BlockSpec(array.shape, lambda j: (0,) * array.ndim)
    return pl.pallas_call(
        functools.partial(aggregate_kernel, rows_step),
        grid=(parents // group,),
        in_specs=[
            pl.BlockSpec((8 * group, 2, depth, width), lambda j: (j, 0, 0, 0)),
            whole(polar3),
            whole(azimuth2),
            whole(azimuth_low),
            whole(trig),
        ],
        out_specs=[pl.BlockSpec((group, 2, depth, fine), lambda j: (j, 0, 0, 0))]
        * (owners + 1),
        out_shape=[jax.ShapeDtypeStruct((parents, 2, depth, fine), jnp.float32)]
        * (owners + 1),
        scratch_shapes=[
            pltpu.VMEM((8, odd_rows + depth, fine), jnp.float32),
            pltpu.VMEM((8, 2, 3 * depth, fine), jnp.bfloat16),
        ],
        cost_estimate=pl.CostEstimate(
            flops=boxes * 2 * depth * fine * width * 24,
            bytes_accessed=3 * boxes * 2 * depth * width * 4,
            transcendentals=0,
        ),
        name="aggregate_parts",
    )(children, polar3, azimuth2, azimuth_low, trig)


def aggregate_constants(depth, width):
    owners = lax.axis_size("dir")
    me = lax.axis_index("dir")
    samples = owners * depth
    fine_polar, fine = 2 * samples, 2 * width
    mine = me * depth
    odd = 2 * ((iota(samples) + mine) % samples) + 1
    even = 2 * (mine + iota(depth))
    polar_high, polar_low = split_bf16(interp_entries(odd, mine + iota(depth), samples))
    polar3 = jnp.concatenate([polar_high, polar_low, polar_high], axis=1)
    azimuth_high, azimuth_low = split_bf16(interp_entries(iota(fine), iota(width), width).T)
    azimuth2 = jnp.concatenate([azimuth_high, azimuth_high], axis=0)
    rows = jnp.concatenate([odd, even])
    polar = (jnp.pi * (rows.astype(jnp.float32) + 0.5) / fine_polar)[:, None]
    azimuth = (2.0 * jnp.pi * iota(fine).astype(jnp.float32) / fine)[None, :]
    wavenumber = fine_polar / 8.0
    x = wavenumber * (jnp.sin(polar) * jnp.cos(azimuth))
    y = wavenumber * (jnp.sin(polar) * jnp.sin(azimuth))
    z = wavenumber * jnp.cos(polar) + jnp.zeros_like(azimuth)
    trig = jnp.stack([jnp.cos(x), jnp.sin(x), jnp.cos(y), jnp.sin(y), jnp.cos(z), jnp.sin(z)])
    return polar3, azimuth2, azimuth_low, trig


def merge_kernel(count, *refs):
    even, terms, out, tiles = refs[0], refs[1 : 1 + count], refs[-2], refs[-1]
    parents, _, depth, fine = even.shape
    for parent in range(parents):
        for part in range(2):
            for lane in range(0, fine, 128):
                columns = slice(lane, lane + 128)
                total = terms[0][parent, part, :, columns]
                for term in terms[1:]:
                    total = total + term[parent, part, :, columns]
                tile = tiles.at[(parent * 2 + part) * (fine // 128) + lane // 128]
                tile[pl.ds(0, depth, stride=2), :] = even[parent, part, :, columns]
                tile[pl.ds(1, depth, stride=2), :] = total
                out[parent, part, :, columns] = tile[...]


def merge(even, terms, after):
    parents, _, depth, fine = even.shape
    group = max(1, parents // 4)
    piece = pl.BlockSpec((group, 2, depth, fine), lambda j: (j, 0, 0, 0))
    return pl.pallas_call(
        functools.partial(merge_kernel, len(terms)),
        grid=(parents // group,),
        in_specs=[piece] * (1 + len(terms)) + [pl.BlockSpec(memory_space=pl.ANY)] * len(after),
        out_specs=pl.BlockSpec((group, 2, 2 * depth, fine), lambda j: (j, 0, 0, 0)),
        out_shape=jax.ShapeDtypeStruct((parents, 2, 2 * depth, fine), jnp.float32),
        scratch_shapes=[pltpu.VMEM((group * 2 * (fine // 128), 2 * depth, 128), jnp.float32)],
        cost_estimate=pl.CostEstimate(
            flops=even.size * len(terms), bytes_accessed=7 * even.size * 4, transcendentals=0
        ),
        name="merge",
    )(even, *terms, *after)


def exchange(odd):
    owners = len(odd)
    if owners != 4:
        send = jnp.stack(odd)
        send = jnp.roll(send, lax.axis_index("dir"), axis=0)
        received = lax.all_to_all(send, "dir", split_axis=0, concat_axis=0, tiled=True)
        return [received[i] for i in range(owners)]
    own, following, opposite, preceding = odd
    from_first = lax.ppermute(preceding, "dir", [(0, 1)])
    from_last = lax.ppermute(following, "dir", [(3, 2)])
    up = lax.ppermute(following, "dir", [(0, 1), (1, 2), (2, 3)])
    down = lax.ppermute(preceding, "dir", [(1, 0), (2, 1), (3, 2)])
    outer = lax.ppermute(opposite, "dir", [(0, 2), (3, 1)])
    passed_on = opposite + (from_first + from_last)
    inner = lax.ppermute(passed_on, "dir", [(1, 3), (2, 0)])
    return [own, up, down, outer, inner]


def translate_kernel(
    rows_step, slots, first, src, cls, before, own, after, table, out, sources, factors, sems
):
    block = own.shape[0]
    classes = table.shape[0]
    boxes, _, depth, _ = out.shape

    @pl.when(pl.program_id(0) == 0)
    def _():
        copies = [
            pltpu.make_async_copy(before, sources.at[pl.ds(0, block)], sems.at[0]),
            pltpu.make_async_copy(own, sources.at[pl.ds(block, block)], sems.at[1]),
            pltpu.make_async_copy(after, sources.at[pl.ds(2 * block, block)], sems.at[2]),
            pltpu.make_async_copy(table, factors.at[pl.ds(0, classes)], sems.at[3]),
        ]
        for copy in copies:
            copy.start()
        factors[classes] = jnp.zeros(table.shape[1:], jnp.float32)
        for copy in copies:
            copy.wait()

    base = pl.program_id(0) * boxes

    def one_box(box, _):
        picks = []
        for slot in range(slots):
            at = (base + box) * slots + slot
            source = src[at]
            empty = source < 0
            picks.append(
                (
                    jnp.where(empty, block, source - first[0]),
                    jnp.where(empty, classes, cls[at]),
                )
            )
        for row in range(0, depth, rows_step):
            rows = slice(row, row + rows_step)
            real, imag = None, None
            for position, operator in picks:
                p_re = sources[position, 0, rows, :]
                p_im = sources[position, 1, rows, :]
                q_re = factors[operator, 0, rows, :]
                q_im = factors[operator, 1, rows, :]
                new_re = q_re * p_re - q_im * p_im
                new_im = q_re * p_im + q_im * p_re
                real = new_re if real is None else real + new_re
                imag = new_im if imag is None else imag + new_im
            out[box, 0, rows, :] = real
            out[box, 1, rows, :] = imag
        return 0

    lax.fori_loop(0, boxes, one_box, 0)


def translate(before, own, after, far_src, far_class, table):
    block, _, depth, width = own.shape
    slots = far_src.shape[1]
    classes = table.shape[0]
    steps = min(8, block)
    boxes = block // steps
    rows_step = max(8, min(depth, 4096 // width))
    first = jnp.reshape((lax.axis_index("box") - 1) * block, (1,)).astype(jnp.int32)
    hbm = pl.BlockSpec(memory_space=pl.ANY)
    return pl.pallas_call(
        functools.partial(translate_kernel, rows_step, slots),
        grid_spec=pltpu.PrefetchScalarGridSpec(
            num_scalar_prefetch=3,
            grid=(steps,),
            in_specs=[hbm] * 4,
            out_specs=pl.BlockSpec((boxes, 2, depth, width), lambda i, *_: (i, 0, 0, 0)),
            scratch_shapes=[
                pltpu.VMEM((3 * block, 2, depth, width), jnp.float32),
                pltpu.VMEM((classes + 1, 2, depth, width), jnp.float32),
                pltpu.SemaphoreType.DMA((4,)),
            ],
        ),
        out_shape=jax.ShapeDtypeStruct(own.shape, jnp.float32),
        cost_estimate=pl.CostEstimate(
            flops=own.size * slots * 4, bytes_accessed=4 * own.size * 4, transcendentals=0
        ),
        name="translate",
    )(first, far_src.reshape(-1), far_class.reshape(-1), before, own, after, table)


def halo(block):
    size = lax.axis_size("box")
    up = [(i, i + 1) for i in range(size - 1)]
    down = [(j, i) for i, j in up]
    before = lax.ppermute(block, "box", up)
    after = lax.ppermute(block, "box", down)
    return before, after


def on_device(
    low_field,
    far_src_low,
    far_class_low,
    table_low,
    far_src_mid,
    far_class_mid,
    table_mid,
    far_src_top,
    far_class_top,
    table_top,
):
    depth, width = low_field.shape[2:]
    low_odd = aggregate_parts(low_field, aggregate_constants(depth, width))
    low_before, low_after = halo(low_field)
    terms = exchange(low_odd[:-1])
    mid_field = merge(low_odd[-1], terms, ())
    mid_odd = aggregate_parts(mid_field, aggregate_constants(2 * depth, 2 * width))
    mid_before, mid_after = halo(mid_field)
    terms = exchange(mid_odd[:-1])
    incoming_low = translate(
        low_before, low_field, low_after, far_src_low, far_class_low, table_low
    )
    top_field = merge(mid_odd[-1], terms, (incoming_low,))
    top_before, top_after = halo(top_field)
    incoming_mid = translate(
        mid_before, mid_field, mid_after, far_src_mid, far_class_mid, table_mid
    )
    incoming_top = translate(
        top_before, top_field, top_after, far_src_top, far_class_top, table_top
    )
    return (incoming_low, incoming_mid, incoming_top)


def solution(mesh):
    in_specs = (
        P("box", None, "dir", None),
        P("box", None),
        P("box", None),
        P(None, None, "dir", None),
        P("box", None),
        P("box", None),
        P(None, None, "dir", None),
        P("box", None),
        P("box", None),
        P(None, None, "dir", None),
    )
    out_specs = (
        P("box", None, "dir", None),
        P("box", None, "dir", None),
        P("box", None, "dir", None),
    )
    return jax.shard_map(
        on_device, mesh=mesh, in_specs=in_specs, out_specs=out_specs, check_vma=False
    )
```
